512 devices in a mesh: seq: 64 (over z, x_lo, core), fsdp: 8 (over y, x_hi).
Axes of the slice: x: 4 (x_hi: 2, x_lo: 2; x = x_hi * 2 + x_lo), y: 4, z: 16, core: 2. Of those that a mesh axis runs over, the one named last changes fastest.
Arguments:
- q_s: bfloat16 [8, 64, 128, 1536], P('fsdp', 'seq'), may hold values from -48 to 48, as said below
- k_s: bfloat16 [8, 64, 128, 1536], P('fsdp', 'seq'), may hold values from -6 to 6, as said below
- v_s: bfloat16 [8, 64, 128, 1536], P('fsdp', 'seq'), may hold values from -6 to 6
- time_index: int32 [8], P('fsdp'), may hold values from 0 to 63
- ada_table: float32 [64, 2, 1536], replicated, may hold values from -3 to 3
- w_temporal: bfloat16 [1536, 4608], P('seq', 'fsdp'), may hold values from -0.15625 to 0.15625
Outputs:
- temporal_out: bfloat16 [8, 64, 128, 1536], P('fsdp', 'seq')
The draws below stay inside these ranges and needn't reach their ends.
Inputs may be any that keep to these rules, and one draw needn't show every extreme that they name: `q_s`: real-valued entries. `k_s`: real-valued entries.
All inputs are finite; a program needn't handle non-finite values.
Results may differ from the reference program's by a relative error of at most 0.015.
Values may be sent and summed in bfloat16 or wider, within the bound.
No kernel may reach another device: no remote copies, remote signals or barrier semaphores. Data moves between devices by JAX's collectives and lax.ppermute only.
A program may use at most 64 MiB of HBM per device.

```python
import jax
import jax.numpy as jnp
from jax import lax

HEADS = 12
HEAD_SIZE = 128
TSTEPS = 64
ITERS = 3
FRAMES = 64
POS = 128
VIDEOS = 8


def query_key_pair(key):
    shape = (VIDEOS, FRAMES, POS, HEADS * HEAD_SIZE)
    first, second = jax.random.split(jax.random.fold_in(key, 7), 2)
    key_rows = jnp.clip(jax.random.normal(first, shape, jnp.float32), -6.0, 6.0)
    query_rows = jnp.clip(jax.random.normal(second, shape, jnp.float32), -6.0, 6.0)
    return (query_rows, key_rows)


def draw_q_s(key, part):
    return query_key_pair(key)[0].astype(jnp.bfloat16)


def draw_k_s(key, part):
    return query_key_pair(key)[1].astype(jnp.bfloat16)


def set_ends(entries, stream_key, smallest, top_value):
    shape = entries.shape
    spot = [jax.random.randint(jax.random.fold_in(stream_key, axis), (), 0, shape[axis]) for axis in range(len(shape))]
    entries = entries.at[tuple(spot)].set(smallest)
    longest = shape.index(max(shape))
    spot[longest] = (spot[longest] + 1) % shape[longest]
    return entries.at[tuple(spot)].set(top_value)


def block_scale(key, shape, pieces, least, top_value):
    def one(position, parts):
        draws = jax.random.uniform(jax.random.fold_in(jax.random.fold_in(key, 6), position), (parts,), jnp.float32, least / len(pieces), top_value / len(pieces))
        return jnp.repeat(jnp.exp(draws), shape[position] // parts).reshape((-1,) + (1,) * (len(shape) - position - 1))

    factor_of = one(*pieces[0])
    for cut in pieces[1:]:
        factor_of = factor_of * one(*cut)
    return factor_of


def bell_draw(key, dims, deviation, reach, shards=(), dtype=jnp.bfloat16):
    values = jax.random.normal(key, dims, jnp.float32) * deviation
    if len(shards) > 0:
        values = block_scale(key, dims, shards, -0.22, 0.18) * values
    return jnp.clip(values, min=-reach, max=reach).astype(dtype)


def setup_inputs(seed: int = 0) -> dict:
    key_of = jax.random.split(jax.random.key(seed), 7)
    q_s = draw_q_s(jax.random.fold_in(key_of[6], 71), 0)
    k_s = draw_k_s(jax.random.fold_in(key_of[6], 71), 0)
    v_s = bell_draw(key_of[2], (VIDEOS, FRAMES, POS, HEADS * HEAD_SIZE), 1.0, 6.0, ((0, 8), (1, 64)))
    time_index = set_ends(jax.random.randint(key_of[3], (VIDEOS,), 0, TSTEPS), jax.random.fold_in(key_of[3], 1), 0, TSTEPS - 1).astype(jnp.int32)
    ada_table = bell_draw(key_of[4], (TSTEPS, 2, HEADS * HEAD_SIZE), 0.5, 3.0, (), jnp.float32)
    w_temporal = bell_draw(key_of[5], (HEADS * HEAD_SIZE, 3 * HEADS * HEAD_SIZE), (HEADS * HEAD_SIZE) ** -0.5, 0.15625, ((0, 64), (1, 8)))
    return {"q_s": q_s, "k_s": k_s, "v_s": v_s, "time_index": time_index, "ada_table": ada_table, "w_temporal": w_temporal}


relax_power = 0.8
norm_eps = 1e-06

def balanced_transport(logit_scores):
    potential_col = jnp.zeros_like(logit_scores[..., :1, :])
    potential_row = jnp.zeros_like(logit_scores[..., :, :1])
    for turn in range(ITERS):
        potential_row = -relax_power * jax.nn.logsumexp(logit_scores + potential_col, axis=-1, keepdims=True)
        potential_col = -relax_power * jax.nn.logsumexp(logit_scores + potential_row, axis=-2, keepdims=True)
    return jnp.exp(logit_scores + potential_row + potential_col).astype(jnp.bfloat16)

def attend(query_rows, key_rows, value_rows):
    count = query_rows.shape[0]
    query_head_split = query_rows.reshape(count, HEADS, HEAD_SIZE).astype(jnp.float32)
    key_head_split = key_rows.reshape(key_rows.shape[0], HEADS, HEAD_SIZE).astype(jnp.float32)
    value_head_split = value_rows.reshape(value_rows.shape[0], HEADS, HEAD_SIZE).astype(jnp.float32)
    logit_scores = jnp.einsum('pgl,bgl->gpb', query_head_split, key_head_split) * (1.0 / HEAD_SIZE ** 0.5)
    transport_plan = balanced_transport(logit_scores)
    attention_output = jnp.einsum('bzg,gbq->zbq', transport_plan.astype(jnp.float32), value_head_split)
    return attention_output.reshape(count, HEADS * HEAD_SIZE).astype(jnp.bfloat16)

def one_video(inputs, ada_table, w_temporal):
    query_rows, key_rows, value_rows, step_index = inputs
    width = HEADS * HEAD_SIZE
    spatial_result = lax.map(lambda frame: attend(frame[0], frame[1], frame[2]), (query_rows, key_rows, value_rows))
    modulate = ada_table[step_index]
    hidden = spatial_result.astype(jnp.float32)
    scaled = hidden * lax.rsqrt(lax.optimization_barrier(jnp.mean(hidden * hidden, axis=-1, keepdims=True)) + norm_eps)
    modulated = (scaled * (1.0 + modulate[0]) + modulate[1]).astype(jnp.bfloat16)
    frames, positions = (modulated.shape[0], modulated.shape[1])
    triple = jnp.dot(modulated.reshape(frames * positions, width), w_temporal, preferred_element_type=jnp.float32)
    triple = triple.astype(jnp.bfloat16).reshape(frames, positions, 3 * width)
    triple = jnp.transpose(triple, (1, 0, 2))
    temporal = lax.map(lambda column: attend(column[:, :width], column[:, width:2 * width], column[:, 2 * width:]), triple)
    return jnp.transpose(temporal, (1, 0, 2))

def reference(q_s, k_s, v_s, time_index, ada_table, w_temporal):
    return lax.map(lambda inputs: one_video(inputs, ada_table, w_temporal), (q_s, k_s, v_s, time_index))
```

```python
import functools
import jax
import jax.numpy as jnp
from jax import lax
from jax.experimental import pallas as pl
from jax.experimental.pallas import tpu as pltpu
from jax.sharding import Mesh, PartitionSpec as P
HEADS=12; HEAD_SIZE=128; ITERS=3; POWER=0.8; EPS=1e-6

def transport(scores):
    col = None
    for _ in range(ITERS):
        shifted = scores if col is None else scores + col
        top = jnp.max(shifted, axis=-1, keepdims=True)
        row = -POWER * (top + jnp.log(jnp.sum(jnp.exp(shifted - top), axis=-1, keepdims=True)))
        shifted = scores + row
        top = jnp.max(shifted, axis=-2, keepdims=True)
        col = -POWER * (top + jnp.log(jnp.sum(jnp.exp(shifted - top), axis=-2, keepdims=True)))
    return jnp.exp(shifted + col).astype(jnp.bfloat16)

def spatial_kernel(group, idx_ref, q_ref, k_ref, v_ref, ada_ref, o_ref, acc_ref):
    step = pl.program_id(0)
    scale = 1.0 / HEAD_SIZE**0.5
    scores = []
    for h in range(group):
        lanes = slice(h*HEAD_SIZE,(h+1)*HEAD_SIZE)
        scores.append(lax.dot_general(q_ref[0,0,:,lanes], k_ref[0,0,:,lanes], (((1,),(1,)),((),())), preferred_element_type=jnp.float32)*scale)
    plan = transport(jnp.stack(scores))
    for h in range(group):
        lanes = slice(h*HEAD_SIZE,(h+1)*HEAD_SIZE)
        out = jnp.dot(plan[h], v_ref[0,0,:,lanes], preferred_element_type=jnp.float32).astype(jnp.bfloat16)
        acc_ref[step, :, lanes] = out
    @pl.when(step == pl.num_programs(0)-1)
    def _():
        n = HEADS//group
        total = None
        for s in range(n):
            part = acc_ref[s].astype(jnp.float32)
            part = jnp.sum(part*part, axis=-1, keepdims=True)
            total = part if total is None else total + part
        inv = lax.rsqrt(total/(HEADS*HEAD_SIZE) + EPS)
        w = group*HEAD_SIZE
        for s in range(n):
            part = acc_ref[s].astype(jnp.float32)
            o_ref[:, s*w:(s+1)*w] = (part*inv*(1.0+ada_ref[0,0:1,s*w:(s+1)*w])+ada_ref[0,1:2,s*w:(s+1)*w]).astype(jnp.bfloat16)

def spatial(idx, q, k, v, ada, group=3):
    width=HEADS*HEAD_SIZE; pos=q.shape[2]
    blk = pl.BlockSpec((1,1,pos,group*HEAD_SIZE), lambda i, idx: (0,0,0,i))
    return pl.pallas_call(
        functools.partial(spatial_kernel, group),
        out_shape=jax.ShapeDtypeStruct((pos,width), jnp.bfloat16),
        grid_spec=pltpu.PrefetchScalarGridSpec(
            num_scalar_prefetch=1, grid=(HEADS//group,),
            in_specs=[blk,blk,blk,pl.BlockSpec((1,2,width), lambda i, idx: (idx[0],0,0))],
            out_specs=pl.BlockSpec((pos,width), lambda i, idx: (0,0)),
            scratch_shapes=[pltpu.VMEM((HEADS//group,pos,group*HEAD_SIZE), jnp.bfloat16)]),
        compiler_params=pltpu.CompilerParams(dimension_semantics=("arbitrary",)),
        cost_estimate=pl.CostEstimate(flops=2*2*12*128*128*128, transcendentals=12*7*128*128, bytes_accessed=4*128*1536*2),
        name="spatial",
    )(idx, q, k, v, ada)

def temporal_kernel(heads, positions, x_ref, w_ref, o_ref):
    scale = 1.0 / HEAD_SIZE**0.5
    width = heads*HEAD_SIZE
    triple = jnp.dot(x_ref[0], w_ref[...], preferred_element_type=jnp.float32).astype(jnp.bfloat16)
    n = triple.shape[0]
    same = (lax.broadcasted_iota(jnp.int32,(n,n),0) % positions) == (lax.broadcasted_iota(jnp.int32,(n,n),1) % positions)
    scores=[]
    for h in range(heads):
        q = triple[:, h*HEAD_SIZE:(h+1)*HEAD_SIZE]
        k = triple[:, width+h*HEAD_SIZE:width+(h+1)*HEAD_SIZE]
        s = lax.dot_general(q,k,(((1,),(1,)),((),())),preferred_element_type=jnp.float32)*scale
        scores.append(jnp.where(same, s, -1e30))
    plan = transport(jnp.stack(scores))
    for h in range(heads):
        v = triple[:, 2*width+h*HEAD_SIZE:2*width+(h+1)*HEAD_SIZE]
        o_ref[0,:,h*HEAD_SIZE:(h+1)*HEAD_SIZE] = jnp.dot(plan[h], v, preferred_element_type=jnp.float32).astype(jnp.bfloat16)

def temporal(x, w, heads, positions):
    vids,n,width=x.shape
    return pl.pallas_call(
        functools.partial(temporal_kernel, heads, positions),
        out_shape=jax.ShapeDtypeStruct((vids,n,heads*HEAD_SIZE), jnp.bfloat16),
        grid=(vids,),
        in_specs=[pl.BlockSpec((1,n,width), lambda i:(i,0,0)), pl.BlockSpec(w.shape, lambda i:(0,0))],
        out_specs=pl.BlockSpec((1,n,heads*HEAD_SIZE), lambda i:(i,0,0)),
        compiler_params=pltpu.CompilerParams(dimension_semantics=("arbitrary",)),
        cost_estimate=pl.CostEstimate(flops=2*vids*n*width*3*heads*HEAD_SIZE, transcendentals=12*7*128*128, bytes_accessed=6*1024*1024),
        name="temporal",
    )(x, w)


UNIT = 192
PIECES = 3


def gather_weights(w):
    rows = w.shape[0]
    source = lax.axis_index("y") * 2 + lax.axis_index("xh")
    units = w.reshape(rows, PIECES, UNIT).transpose(1, 0, 2)
    ring = jnp.concatenate([units, jnp.zeros((8 - PIECES, rows, UNIT), w.dtype)], axis=0)
    ring = jnp.concatenate([ring, ring], axis=0)
    slots = lax.dynamic_slice_in_dim(ring, (-PIECES * source) % 8, 8, axis=0)
    slots = slots.reshape(1, 4, 1, 2, rows, UNIT)
    slots = jnp.broadcast_to(slots, (4, 4, 2, 2, rows, UNIT)).reshape(32, 2, rows, UNIT)
    slots = lax.all_to_all(slots, ("xl", "c", "y", "xh"), split_axis=0, concat_axis=0, tiled=True)
    slots = slots.reshape(2, 2, 8, 2, rows, UNIT)
    mine = lax.dynamic_index_in_dim(slots, lax.axis_index("c"), 0, keepdims=False)
    target = 2 * lax.axis_index("y")
    columns = []
    for part in range(3):
        for half in range(2):
            owner = (target + half + 8 * part) // PIECES
            columns.append(lax.dynamic_index_in_dim(mine[:, :, half], owner, 1, keepdims=False))
    block = jnp.concatenate(columns, axis=-1).reshape(2 * rows, 6 * UNIT)
    return lax.all_gather(block, ("z", "c"), axis=0, tiled=True)


def local(q_s, k_s, v_s, time_index, ada_table, w_temporal):
    width = HEADS * HEAD_SIZE
    weights = gather_weights(w_temporal)
    modulated = spatial(time_index, q_s, k_s, v_s, ada_table, 6)
    relayed = lax.all_to_all(modulated.reshape(64, 2, width), ("z", "xl", "c"), split_axis=0, concat_axis=0, tiled=True)
    relayed = jnp.broadcast_to(relayed.reshape(1, 128, width), (4, 128, width))
    tokens = lax.all_to_all(relayed, "y", split_axis=0, concat_axis=0, tiled=True)
    out = temporal(tokens, weights, 3, 2)
    out = out.reshape(4, 64, 2, 384).transpose(1, 0, 2, 3).reshape(256, 2, 384)
    out = lax.all_to_all(out, ("z", "xl", "c", "y"), split_axis=0, concat_axis=0, tiled=True)
    out = out.reshape(64, 4, 2, 384).transpose(0, 2, 1, 3)
    return out.reshape(1, 1, 128, width)


def solution(mesh):
    fine = Mesh(mesh.devices.reshape(16, 2, 2, 4, 2), ("z", "xl", "c", "y", "xh"))
    seq, fsdp = ("z", "xl", "c"), ("y", "xh")
    frames = P(fsdp, seq, None, None)
    in_specs = (frames, frames, frames, P(fsdp), P(), P(seq, fsdp))
    return jax.shard_map(local, mesh=fine, in_specs=in_specs, out_specs=frames, check_vma=False)
```

```python
import functools
import jax
import jax.numpy as jnp
from jax import lax
from jax.experimental import pallas as pl
from jax.experimental.pallas import tpu as pltpu
from jax.sharding import Mesh, PartitionSpec as P
HEADS=12; HEAD_SIZE=128; ITERS=3; POWER=0.8; EPS=1e-6


def transport(scores):
    col = None
    for _ in range(ITERS):
        shifted = scores if col is None else scores + col
        top = jnp.max(shifted, axis=-1, keepdims=True)
        row = -POWER * (top + jnp.log(jnp.sum(jnp.exp(shifted - top), axis=-1, keepdims=True)))
        shifted = scores + row
        top = jnp.max(shifted, axis=-2, keepdims=True)
        col = -POWER * (top + jnp.log(jnp.sum(jnp.exp(shifted - top), axis=-2, keepdims=True)))
    return jnp.exp(shifted + col).astype(jnp.bfloat16)


def spatial_kernel(group, idx_ref, q_ref, k_ref, v_ref, ada_ref, o_ref, acc_ref):
    step = pl.program_id(0)
    scale = 1.0 / HEAD_SIZE**0.5
    scores = []
    for h in range(group):
        lanes = slice(h*HEAD_SIZE,(h+1)*HEAD_SIZE)
        scores.append(lax.dot_general(q_ref[0,0,:,lanes], k_ref[0,0,:,lanes], (((1,),(1,)),((),())), preferred_element_type=jnp.float32)*scale)
    plan = transport(jnp.stack(scores))
    for h in range(group):
        lanes = slice(h*HEAD_SIZE,(h+1)*HEAD_SIZE)
        out = jnp.dot(plan[h], v_ref[0,0,:,lanes], preferred_element_type=jnp.float32).astype(jnp.bfloat16)
        acc_ref[step, :, lanes] = out

    @pl.when(step == pl.num_programs(0)-1)
    def _():
        n = HEADS//group
        total = None
        for s in range(n):
            part = acc_ref[s].astype(jnp.float32)
            part = jnp.sum(part*part, axis=-1, keepdims=True)
            total = part if total is None else total + part
        inv = lax.rsqrt(total/(HEADS*HEAD_SIZE) + EPS)
        w = group*HEAD_SIZE
        for s in range(n):
            part = acc_ref[s].astype(jnp.float32)
            o_ref[:, s*w:(s+1)*w] = (part*inv*(1.0+ada_ref[0,0:1,s*w:(s+1)*w])+ada_ref[0,1:2,s*w:(s+1)*w]).astype(jnp.bfloat16)


def spatial(idx, q, k, v, ada, group=3):
    width=HEADS*HEAD_SIZE; pos=q.shape[2]
    blk = pl.BlockSpec((1,1,pos,group*HEAD_SIZE), lambda i, idx: (0,0,0,i))
    return pl.pallas_call(
        functools.partial(spatial_kernel, group),
        out_shape=jax.ShapeDtypeStruct((pos,width), jnp.bfloat16),
        grid_spec=pltpu.PrefetchScalarGridSpec(
            num_scalar_prefetch=1, grid=(HEADS//group,),
            in_specs=[blk,blk,blk,pl.BlockSpec((1,2,width), lambda i, idx: (idx[0],0,0))],
            out_specs=pl.BlockSpec((pos,width), lambda i, idx: (0,0)),
            scratch_shapes=[pltpu.VMEM((HEADS//group,pos,group*HEAD_SIZE), jnp.bfloat16)]),
        compiler_params=pltpu.CompilerParams(dimension_semantics=("arbitrary",)),
        cost_estimate=pl.CostEstimate(flops=2*2*12*128*128*128, transcendentals=12*7*128*128, bytes_accessed=4*128*1536*2),
        name="spatial",
    )(idx, q, k, v, ada)


def temporal_kernel(positions, here_ref, x_ref, *refs):
    blocks, o_ref, w_ref, sem = refs[:8], refs[8], refs[9], refs[10]
    x_here, c_here = here_ref[0], here_ref[1]

    def copy(i):
        far = lax.rem(x_here + 4 - i // 2, 4)
        core = lax.rem(c_here + i % 2, 2)
        return pltpu.make_async_copy(blocks[i], w_ref.at[lax.div(far, 2), :, lax.rem(far, 2), core], sem.at[i])

    @pl.when(pl.program_id(0) == 0)
    def _():
        for i in range(8):
            copy(i).start()
        for i in range(8):
            copy(i).wait()

    scale = 1.0 / HEAD_SIZE**0.5
    vids, n, width = o_ref.shape[0], x_ref.shape[1], x_ref.shape[2]
    x = x_ref[pl.ds(pl.program_id(0) * vids, vids)].reshape(vids * n, width)
    whole = w_ref.reshape(2, width, w_ref.shape[-1])
    part = [jnp.dot(x, whole[e], preferred_element_type=jnp.float32).astype(jnp.bfloat16) for e in range(2)]
    full, half = HEAD_SIZE, HEAD_SIZE // 2
    triple = []
    for j in range(3):
        first = part[0][:, j * full:(j + 1) * full]
        last = part[1][:, j * full:(j + 1) * full]
        cut = slice(3 * full + j * half, 3 * full + (j + 1) * half)
        middle = jnp.concatenate([part[0][:, cut], part[1][:, cut]], axis=-1)
        triple.append((first, middle, last))
    same = (lax.broadcasted_iota(jnp.int32, (n, n), 0) % positions) == (lax.broadcasted_iota(jnp.int32, (n, n), 1) % positions)
    scores = []
    for b in range(vids):
        for h in range(3):
            rows = slice(b * n, (b + 1) * n)
            s = lax.dot_general(triple[0][h][rows], triple[1][h][rows], (((1,), (1,)), ((), ())), preferred_element_type=jnp.float32) * scale
            scores.append(jnp.where(same, s, -1e30))
    plan = transport(jnp.stack(scores))
    for b in range(vids):
        for h in range(3):
            rows = slice(b * n, (b + 1) * n)
            o_ref[b, :, h * full:(h + 1) * full] = jnp.dot(plan[b * 3 + h], triple[2][h][rows], preferred_element_type=jnp.float32).astype(jnp.bfloat16)


def temporal(here, x, blocks, positions, group):
    vids, n, width = x.shape
    cols = 3 * HEAD_SIZE
    z, rows, piece = blocks[0].shape
    return pl.pallas_call(
        functools.partial(temporal_kernel, positions),
        out_shape=jax.ShapeDtypeStruct((vids, n, cols), jnp.bfloat16),
        grid_spec=pltpu.PrefetchScalarGridSpec(
            num_scalar_prefetch=1,
            grid=(vids // group,),
            in_specs=[pl.BlockSpec(memory_space=pltpu.VMEM)] + [pl.BlockSpec(memory_space=pltpu.HBM)] * 8,
            out_specs=pl.BlockSpec((group, n, cols), lambda i, here: (i, 0, 0)),
            scratch_shapes=[pltpu.VMEM((2, z, 2, 2, rows, piece), jnp.bfloat16), pltpu.SemaphoreType.DMA((8,))]),
        compiler_params=pltpu.CompilerParams(dimension_semantics=("arbitrary",), vmem_limit_bytes=50 * 1024 * 1024),
        cost_estimate=pl.CostEstimate(flops=2 * vids * n * width * 3 * cols, transcendentals=vids * 3 * 7 * n * n, bytes_accessed=6 * 1024 * 1024),
        name="temporal",
    )(here, x, *blocks)


UNIT = 192
PIECES = 3
RING = (0, 2, 1, 3)


def everyone(x, axes, count):
    return lax.all_to_all(jnp.broadcast_to(x[None], (count,) + x.shape), axes, split_axis=0, concat_axis=0, tiled=True)


def gather_weights(w):
    rows = w.shape[0]
    me = lax.axis_index("y") * 2 + lax.axis_index("xh")
    found = []
    for i in range(PIECES):
        found.append(lax.ppermute(w[:, i * UNIT:(i + 1) * UNIT], ("y", "xh"), [(g, (PIECES * g + i) % 8) for g in range(8)]))
    found = jnp.stack(found)
    parts = [lax.dynamic_index_in_dim(found, (me + 8 * part) % PIECES, 0, keepdims=False) for part in range(3)]
    low = lax.axis_index("xh") == 0
    long = [jnp.where(low, p[:, :128], p[:, 64:]) for p in parts]
    short = [jnp.where(low, p[:, 128:], p[:, :64]) for p in parts]
    block = jnp.concatenate(long + short, axis=-1)
    block = lax.all_gather(block, "z", axis=0, tiled=True).reshape(16, rows, 3 * UNIT)
    return block


def spread(block):
    blocks = []
    for shift in range(4):
        near = lax.ppermute(block, ("xl", "xh"), [(RING.index(i), RING.index((i + shift) % 4)) for i in range(4)]) if shift else block
        blocks += [near, lax.ppermute(near, "c", [(0, 1), (1, 0)])]
    return blocks


def local(q_s, k_s, v_s, time_index, ada_table, w_temporal):
    width = HEADS * HEAD_SIZE
    here = jnp.stack([lax.axis_index("xh") * 2 + lax.axis_index("xl"), lax.axis_index("c")])
    weights = spread(gather_weights(w_temporal))
    modulated = spatial(time_index, q_s, k_s, v_s, ada_table, 6)
    modulated, here = lax.optimization_barrier((modulated, here))
    relayed = lax.all_to_all(modulated.reshape(64, 2, width), ("z", "xl", "c"), split_axis=0, concat_axis=0, tiled=True)
    tokens = everyone(relayed.reshape(128, width), "y", 4)
    out = temporal(here, tokens, weights, 2, 2)
    out = out.reshape(4, 64, 2, 384).transpose(1, 0, 2, 3).reshape(256, 2, 384)
    out = lax.all_to_all(out, ("z", "xl", "c", "y"), split_axis=0, concat_axis=0, tiled=True)
    out = out.reshape(64, 4, 2, 384).transpose(0, 2, 1, 3)
    return out.reshape(1, 1, 128, width)


def solution(mesh):
    fine = Mesh(mesh.devices.reshape(16, 2, 2, 4, 2), ("z", "xl", "c", "y", "xh"))
    seq, fsdp = ("z", "xl", "c"), ("y", "xh")
    frames = P(fsdp, seq, None, None)
    in_specs = (frames, frames, frames, P(fsdp), P(), P(seq, fsdp))
    return jax.shard_map(local, mesh=fine, in_specs=in_specs, out_specs=frames, check_vma=False)
```

```python
import functools
import jax
import jax.numpy as jnp
from jax import lax
from jax.experimental import pallas as pl
from jax.experimental.pallas import tpu as pltpu
from jax.sharding import Mesh, PartitionSpec as P
HEADS=12; HEAD_SIZE=128; ITERS=3; POWER=0.8; EPS=1e-6


def transport(scores):
    col = None
    for _ in range(ITERS):
        shifted = scores if col is None else scores + col
        top = jnp.max(shifted, axis=-1, keepdims=True)
        row = -POWER * (top + jnp.log(jnp.sum(jnp.exp(shifted - top), axis=-1, keepdims=True)))
        shifted = scores + row
        top = jnp.max(shifted, axis=-2, keepdims=True)
        col = -POWER * (top + jnp.log(jnp.sum(jnp.exp(shifted - top), axis=-2, keepdims=True)))
    return jnp.exp(shifted + col).astype(jnp.bfloat16)


def spatial_kernel(group, idx_ref, q_ref, k_ref, v_ref, ada_ref, o_ref, acc_ref):
    step = pl.program_id(0)
    scale = 1.0 / HEAD_SIZE**0.5
    scores = []
    for h in range(group):
        lanes = slice(h*HEAD_SIZE,(h+1)*HEAD_SIZE)
        scores.append(lax.dot_general(q_ref[0,0,:,lanes], k_ref[0,0,:,lanes], (((1,),(1,)),((),())), preferred_element_type=jnp.float32)*scale)
    plan = transport(jnp.stack(scores))
    for h in range(group):
        lanes = slice(h*HEAD_SIZE,(h+1)*HEAD_SIZE)
        out = jnp.dot(plan[h], v_ref[0,0,:,lanes], preferred_element_type=jnp.float32).astype(jnp.bfloat16)
        acc_ref[step, :, lanes] = out

    @pl.when(step == pl.num_programs(0)-1)
    def _():
        n = HEADS//group
        total = None
        for s in range(n):
            part = acc_ref[s].astype(jnp.float32)
            part = jnp.sum(part*part, axis=-1, keepdims=True)
            total = part if total is None else total + part
        inv = lax.rsqrt(total/(HEADS*HEAD_SIZE) + EPS)
        w = group*HEAD_SIZE
        for s in range(n):
            part = acc_ref[s].astype(jnp.float32)
            o_ref[:, :, s*w:(s+1)*w] = (part*inv*(1.0+ada_ref[0,0:1,s*w:(s+1)*w])+ada_ref[0,1:2,s*w:(s+1)*w]).astype(jnp.bfloat16).reshape(o_ref.shape[0], o_ref.shape[1], w)


def spatial(idx, q, k, v, ada, group=3):
    width=HEADS*HEAD_SIZE; pos=q.shape[2]
    blk = pl.BlockSpec((1,1,pos,group*HEAD_SIZE), lambda i, idx: (0,0,0,i))
    return pl.pallas_call(
        functools.partial(spatial_kernel, group),
        out_shape=jax.ShapeDtypeStruct((pos//2,2,width), jnp.bfloat16),
        grid_spec=pltpu.PrefetchScalarGridSpec(
            num_scalar_prefetch=1, grid=(HEADS//group,),
            in_specs=[blk,blk,blk,pl.BlockSpec((1,2,width), lambda i, idx: (idx[0],0,0))],
            out_specs=pl.BlockSpec((pos//2,2,width), lambda i, idx: (0,0,0)),
            scratch_shapes=[pltpu.VMEM((HEADS//group,pos,group*HEAD_SIZE), jnp.bfloat16)]),
        compiler_params=pltpu.CompilerParams(dimension_semantics=("arbitrary",)),
        cost_estimate=pl.CostEstimate(flops=2*2*12*128*128*128, transcendentals=12*7*128*128, bytes_accessed=4*128*1536*2),
        name="spatial",
    )(idx, q, k, v, ada)


def temporal_kernel(positions, here_ref, x_ref, *refs):
    blocks, o_ref, w_ref, sem = refs[:8], refs[8], refs[9], refs[10]
    x_here, c_here = here_ref[0], here_ref[1]

    def copy(i):
        far = lax.rem(x_here + 4 - i // 2, 4)
        core = lax.rem(c_here + i % 2, 2)
        return pltpu.make_async_copy(blocks[i], w_ref.at[lax.div(far, 2), :, lax.rem(far, 2), core], sem.at[i])

    @pl.when(pl.program_id(0) == 0)
    def _():
        for i in range(8):
            copy(i).start()
        for i in range(8):
            copy(i).wait()

    scale = 1.0 / HEAD_SIZE**0.5
    vids, n, width = o_ref.shape[0], x_ref.shape[1], x_ref.shape[2]
    x = x_ref[pl.ds(pl.program_id(0) * vids, vids)].reshape(vids * n, width)
    whole = w_ref.reshape(2, width, w_ref.shape[-1])
    part = [jnp.dot(x, whole[e], preferred_element_type=jnp.float32).astype(jnp.bfloat16) for e in range(2)]
    full, half = HEAD_SIZE, HEAD_SIZE // 2
    triple = []
    for j in range(3):
        first = part[0][:, j * full:(j + 1) * full]
        last = part[1][:, j * full:(j + 1) * full]
        cut = slice(3 * full + j * half, 3 * full + (j + 1) * half)
        middle = jnp.concatenate([part[0][:, cut], part[1][:, cut]], axis=-1)
        triple.append((first, middle, last))
    same = (lax.broadcasted_iota(jnp.int32, (n, n), 0) % positions) == (lax.broadcasted_iota(jnp.int32, (n, n), 1) % positions)
    scores = []
    for b in range(vids):
        for h in range(3):
            rows = slice(b * n, (b + 1) * n)
            s = lax.dot_general(triple[0][h][rows], triple[1][h][rows], (((1,), (1,)), ((), ())), preferred_element_type=jnp.float32) * scale
            scores.append(jnp.where(same, s, -1e30))
    plan = transport(jnp.stack(scores))
    for b in range(vids):
        for h in range(3):
            rows = slice(b * n, (b + 1) * n)
            o_ref[b, :, h * full:(h + 1) * full] = jnp.dot(plan[b * 3 + h], triple[2][h][rows], preferred_element_type=jnp.float32).astype(jnp.bfloat16)


def temporal(here, x, blocks, positions, group):
    vids, n, width = x.shape
    cols = 3 * HEAD_SIZE
    z, rows, piece = blocks[0].shape
    return pl.pallas_call(
        functools.partial(temporal_kernel, positions),
        out_shape=jax.ShapeDtypeStruct((vids, n, cols), jnp.bfloat16),
        grid_spec=pltpu.PrefetchScalarGridSpec(
            num_scalar_prefetch=1,
            grid=(vids // group,),
            in_specs=[pl.BlockSpec(memory_space=pltpu.VMEM)] + [pl.BlockSpec(memory_space=pltpu.HBM)] * 8,
            out_specs=pl.BlockSpec((group, n, cols), lambda i, here: (i, 0, 0)),
            scratch_shapes=[pltpu.VMEM((2, z, 2, 2, rows, piece), jnp.bfloat16), pltpu.SemaphoreType.DMA((8,))]),
        compiler_params=pltpu.CompilerParams(dimension_semantics=("arbitrary",), vmem_limit_bytes=51 * 1024 * 1024),
        cost_estimate=pl.CostEstimate(flops=2 * vids * n * width * 3 * cols, transcendentals=vids * 3 * 7 * n * n, bytes_accessed=6 * 1024 * 1024),
        name="temporal",
    )(here, x, *blocks)


UNIT = 192
PIECES = 3
RING = (0, 2, 1, 3)


def everyone(x, axes, count):
    return lax.all_to_all(jnp.broadcast_to(x[None], (count,) + x.shape), axes, split_axis=0, concat_axis=0, tiled=True)


def gather_weights(w):
    rows = w.shape[0]
    me = lax.axis_index("y") * 2 + lax.axis_index("xh")
    found = []
    for i in range(PIECES):
        found.append(lax.ppermute(w[:, i * UNIT:(i + 1) * UNIT], ("y", "xh"), [(g, (PIECES * g + i) % 8) for g in range(8)]))
    found = jnp.stack(found)
    parts = [lax.dynamic_index_in_dim(found, (me + 8 * part) % PIECES, 0, keepdims=False) for part in range(3)]
    low = lax.axis_index("xh") == 0
    long = [jnp.where(low, p[:, :128], p[:, 64:]) for p in parts]
    short = [jnp.where(low, p[:, 128:], p[:, :64]) for p in parts]
    block = jnp.concatenate(long + short, axis=-1)
    block = lax.all_gather(block, "z", axis=0, tiled=True).reshape(16, rows, 3 * UNIT)
    return block


def spread(block):
    blocks = []
    for shift in range(4):
        near = lax.ppermute(block, ("xl", "xh"), [(RING.index(i), RING.index((i + shift) % 4)) for i in range(4)]) if shift else block
        blocks += [near, lax.ppermute(near, "c", [(0, 1), (1, 0)])]
    return blocks


def local(q_s, k_s, v_s, time_index, ada_table, w_temporal):
    width = HEADS * HEAD_SIZE
    here = jnp.stack([lax.axis_index("xh") * 2 + lax.axis_index("xl"), lax.axis_index("c")])
    weights = spread(gather_weights(w_temporal))
    modulated = spatial(time_index, q_s, k_s, v_s, ada_table, 12)
    modulated, here = lax.optimization_barrier((modulated, here))
    relayed = lax.all_to_all(modulated.reshape(64, 2, width), ("z", "xl", "c"), split_axis=0, concat_axis=0, tiled=True)
    tokens = everyone(relayed.reshape(128, width), "y", 4)
    out = temporal(here, tokens, weights, 2, 4)
    out = out.reshape(4, 64, 2, 384).transpose(1, 0, 2, 3).reshape(256, 2, 384)
    out = lax.all_to_all(out, ("z", "xl", "c", "y"), split_axis=0, concat_axis=0, tiled=True)
    out = out.reshape(64, 4, 2, 384).transpose(0, 2, 1, 3)
    return out.reshape(1, 1, 128, width)


def solution(mesh):
    fine = Mesh(mesh.devices.reshape(16, 2, 2, 4, 2), ("z", "xl", "c", "y", "xh"))
    seq, fsdp = ("z", "xl", "c"), ("y", "xh")
    frames = P(fsdp, seq, None, None)
    in_specs = (frames, frames, frames, P(fsdp), P(), P(seq, fsdp))
    return jax.shard_map(local, mesh=fine, in_specs=in_specs, out_specs=frames, check_vma=False)
```
